32 devices in a mesh: vis: 8 (over z, x), tile: 4 (over y, core).
Axes of the slice: x: 2, y: 2, z: 4, core: 2. Of those that a mesh axis runs over, the one named last changes fastest.
Arguments:
- vis_data: bfloat16 [32768, 128], P(('vis', 'tile')), may hold values from -0.59765625 to 0.59765625
- u_cell: int32 [16, 32768], P(None, ('vis', 'tile')), may hold values from 0 to 25
- v_cell: int32 [16, 32768], P(None, ('vis', 'tile')), may hold values from 0 to 25
- u_frac: int32 [16, 32768], P(None, ('vis', 'tile')), may hold values from 0 to 15
- v_frac: int32 [16, 32768], P(None, ('vis', 'tile')), may hold values from 0 to 15
- w_plane: int32 [16, 32768], P(None, ('vis', 'tile')), may hold values from 0 to 7
- block_route: int32 [32768, 1], P(('vis', 'tile')), may hold values from 0 to 63; in each aligned block of 1024 rows (0 to 1023, 1024 to 2047, ...) at most 32 rows name the same one
- kernel_taps: float32 [128, 7], replicated, may hold values from 0.1 to 1
- taper_gain: float32 [32, 32], replicated, may hold values from 0.2 to 1
- sub_tile: int32 [256, 1], P(('vis', 'tile')), may hold values from 0 to 7; in each aligned block of 8 rows (0 to 7, 8 to 15, ...) at most 2 rows name the same one
- sub_anchor: int32 [256, 2], P(('vis', 'tile')), may hold values from 0 to 224
Outputs:
- grid_sum: float32 [8, 256, 2048], P('tile', 'vis')
The draws below stay inside these ranges and needn't reach their ends.
Inputs may be any that keep to these rules, and one draw needn't show every extreme that they name: `block_route`: among the rows of one device at most 32 name one uv-block, and some uv-block is named by exactly 32 of them. `sub_tile`: among the 8 uv-blocks of one device at most 2 map to one grid tile, and some grid tile gets exactly 2 of them.
All inputs are finite; a program needn't handle non-finite values.
Results may differ from the reference program's by a relative error of at most 0.008.
Values may be sent and summed in bfloat16 or wider, within the bound.
A program may use at most 128 MiB of HBM per device.

```python
import math
import jax
import jax.numpy as jnp
import numpy as np
from jax import lax

ROWS_DEV = 1024
BLK_DEV = 8
SUB = 32
CHR = 16
POLC = 8
TAPS = 7
OS = 16
WPL = 8
TS = 256
SCAP = 2
NGROUP = 64
CAP = 32
GT = 8
NROWS = 32768
NBLK = 256
N_VIS = 8
N_TILE = 4
DEVICES = 32


def place_ends(array, key, least, top_value):
    spot = [jax.random.randint(jax.random.fold_in(key, axis), (), 0, length) for axis, length in enumerate(array.shape)]
    widest = array.shape.index(max(array.shape))
    beside = spot[:widest] + [(spot[widest] + 1) % array.shape[widest]] + spot[widest + 1:]
    return array.at[tuple(spot)].set(least).at[tuple(beside)].set(top_value)


def steps_of(own_key, dims, pieces, least, high):
    level, own = 1.0, jax.random.fold_in(own_key, 6)
    for axis_at, parts in pieces:
        steps = jnp.exp(jax.random.uniform(jax.random.fold_in(own, axis_at), (parts,), jnp.float32, least / len(pieces), high / len(pieces)))
        level = level * jnp.repeat(steps, dims[axis_at] // parts).reshape([-1 if axis == axis_at else 1 for axis in range(len(dims))])
    return level


def routed_block(rng, own, number, rows, amount, top, bound, slope):
    ranking = jax.random.permutation(rng, amount)
    heavy_load, ordinary = load_shares(amount, rows * top, bound, slope, True), load_shares(amount, rows * top, bound, slope, False)
    places = jnp.arange(amount)

    def named(tallies, rotation):
        used = int((tallies > 0).sum())
        fixed = max(1, used // 4)
        shifted = fixed + (places - fixed + rotation * (used - fixed)) % max(1, amount - fixed)
        return jnp.zeros((amount,), jnp.int32).at[ranking[jnp.where(places < fixed, places, shifted)]].set(jnp.asarray(tallies, jnp.int32))

    tallies = jnp.where(number % 4 == 0, named(heavy_load, number // 4), named(ordinary, number - number // 4 - 1))
    mixed = jax.random.permutation(jax.random.fold_in(own, 3), amount)
    donor, sink = mixed[0:amount // 2 * 2:2], mixed[1:amount // 2 * 2:2]
    slack = jnp.minimum(tallies[donor] - 1, bound - tallies[sink]) // 2
    slack = jnp.where((donor == ranking[0]) | (sink == ranking[0]) | (tallies[sink] == 0), 0, jnp.maximum(slack, 0))
    shifted = jax.random.randint(jax.random.fold_in(own, 4), (amount // 2,), 0, 1 << 20) % (slack + 1)
    tallies = tallies.at[donor].add(-shifted).at[sink].add(shifted)
    items = jnp.searchsorted(jnp.cumsum(tallies), jnp.arange(rows * top), side="right").astype(jnp.int32)
    grid = items.reshape(top, rows).T
    grid = grid[jax.random.permutation(jax.random.fold_in(own, 1), rows)]
    rotation = jax.random.randint(jax.random.fold_in(own, 2), (rows, 1), 0, top)
    return jnp.take_along_axis(grid, (jnp.arange(top)[None, :] + rotation) % top, axis=1)


def load_shares(number_of, total, bound, skew, full):
    portions = [(1 << 20) // math.isqrt(standing ** skew) + 1 for standing in range(1, number_of + 1)]
    largest = bound if full else min(bound, max(-(-total // number_of), total * portions[0] // sum(portions)))
    least = 1 if total - largest >= number_of - 1 else 0
    holding, surplus = [largest] + [least] * (number_of - 1), total - largest - least * (number_of - 1)
    while surplus > 0:
        candidates = [i for i in range(1, number_of) if holding[i] < largest] or [i for i in range(1, number_of) if holding[i] < bound]
        mass, budget = sum([portions[i] for i in candidates]), surplus
        for i in candidates:
            addition = min(bound - holding[i], max(1, budget * portions[i] // mass), surplus)
            holding[i] = holding[i] + addition
            surplus = surplus - addition
    return np.array(holding)


def centred(key, shape, scale, bound, shards=(), kind=jnp.bfloat16):
    result = scale * jax.random.normal(key, shape, jnp.float32)
    if shards:
        result = result * steps_of(key, shape, shards, -0.22, 0.18)
    return jnp.clip(result, -bound, bound).astype(kind)


def setup_inputs(seed: int = 0) -> dict:
    keys = jax.random.split(jax.random.key(seed), 12)
    vis_data = centred(keys[0], (NROWS, CHR * POLC), 0.1, 0.59765625, ((0, 32),))
    u_cell = place_ends(jax.random.randint(keys[1], (CHR, NROWS), 0, SUB - TAPS + 1), jax.random.fold_in(keys[1], 1), 0, SUB - TAPS).astype(jnp.int32)
    v_cell = place_ends(jax.random.randint(keys[2], (CHR, NROWS), 0, SUB - TAPS + 1), jax.random.fold_in(keys[2], 1), 0, SUB - TAPS).astype(jnp.int32)
    u_frac = place_ends(jax.random.randint(keys[3], (CHR, NROWS), 0, OS), jax.random.fold_in(keys[3], 1), 0, OS - 1).astype(jnp.int32)
    v_frac = place_ends(jax.random.randint(keys[4], (CHR, NROWS), 0, OS), jax.random.fold_in(keys[4], 1), 0, OS - 1).astype(jnp.int32)
    w_plane = place_ends(jax.random.randint(keys[5], (CHR, NROWS), 0, WPL), jax.random.fold_in(keys[5], 1), 0, WPL - 1).astype(jnp.int32)
    block_route_keys = jax.random.split(jax.random.fold_in(keys[6], 1), NROWS // ROWS_DEV)
    block_route_turns = jax.random.permutation(jax.random.fold_in(keys[6], 3), NROWS // ROWS_DEV)
    block_route = jax.vmap(lambda own, number: routed_block(jax.random.fold_in(keys[6], 2), own, number, ROWS_DEV, NGROUP, 1, CAP, 2))(block_route_keys, block_route_turns).reshape((NROWS, 1))
    kernel_taps = jnp.clip(jax.random.uniform(keys[7], (WPL * OS, TAPS), jnp.float32, 0.1, 1.0), 0.1, 1.0)
    taper_gain = jnp.clip(jax.random.uniform(keys[8], (SUB, SUB), jnp.float32, 0.2, 1.0), 0.2, 1.0)
    sub_tile_keys = jax.random.split(jax.random.fold_in(keys[9], 1), NBLK // BLK_DEV)
    sub_tile_turns = jax.random.permutation(jax.random.fold_in(keys[9], 3), NBLK // BLK_DEV)
    sub_tile = jax.vmap(lambda own, number: routed_block(jax.random.fold_in(keys[9], 2), own, number, BLK_DEV, GT, 1, SCAP, 2))(sub_tile_keys, sub_tile_turns).reshape((NBLK, 1))
    sub_anchor = place_ends(jax.random.randint(keys[10], (NBLK, 2), 0, TS - SUB + 1), jax.random.fold_in(keys[10], 1), 0, TS - SUB).astype(jnp.int32)
    return {"vis_data": vis_data, "u_cell": u_cell, "v_cell": v_cell, "u_frac": u_frac, "v_frac": v_frac, "w_plane": w_plane, "block_route": block_route, "kernel_taps": kernel_taps, "taper_gain": taper_gain, "sub_tile": sub_tile, "sub_anchor": sub_anchor}


def spread(cell_idx, taps):
    offset = jnp.arange(SUB, dtype=jnp.int32)[None, :] - cell_idx[:, None]
    spread_sum = jnp.zeros((cell_idx.shape[0], SUB), jnp.float32)
    for tap_index in range(TAPS):
        spread_sum = spread_sum + jnp.where(offset == tap_index, taps[:, tap_index:tap_index + 1], 0.0)
    return spread_sum.astype(jnp.bfloat16)


def grid_block(samples, code_rows, kernel_taps, taper_gain):
    taps_u = kernel_taps[code_rows[2]]
    taps_v = kernel_taps[code_rows[3]]
    weight_u = spread(code_rows[0], taps_u)
    weight_v = spread(code_rows[1], taps_v)
    weighted = (weight_u.astype(jnp.float32)[:, :, None] * samples.astype(jnp.float32)[:, None, :]).astype(jnp.bfloat16)
    weighted = weighted.reshape(samples.shape[0], SUB * POLC)
    subgrid = jnp.dot(weight_v.T, weighted, preferred_element_type=jnp.float32)
    return subgrid * jnp.repeat(taper_gain, POLC, axis=1)


def place_tiles(canvas, sub_grids, tile_ids, anchors, first_tile):
    tile_count = canvas.shape[0]

    def add_one(slot_index, canvas):
        target = (tile_ids[slot_index] - first_tile).astype(jnp.int32)
        inside = (target >= 0) & (target < tile_count)
        target = jnp.clip(target, 0, tile_count - 1).astype(jnp.int32)
        corner = (target, anchors[slot_index, 0].astype(jnp.int32), (anchors[slot_index, 1] * POLC).astype(jnp.int32))
        window = lax.dynamic_slice(canvas, corner, (1, SUB, SUB * POLC))
        addend = jnp.where(inside, sub_grids[slot_index], 0.0)[None]
        return lax.dynamic_update_slice(canvas, window + addend, corner)

    return lax.fori_loop(0, sub_grids.shape[0], add_one, canvas)


def rank_rows(row_route):
    onehot = (row_route[:, None] == jnp.arange(NGROUP, dtype=jnp.int32)[None, :]).astype(jnp.int32)
    before = jnp.cumsum(onehot, axis=0) - onehot
    return jnp.sum(before * onehot, axis=1).astype(jnp.int32)


def reference(vis_data, u_cell, v_cell, u_frac, v_frac, w_plane, block_route, kernel_taps, taper_gain, sub_tile, sub_anchor):
    flat_route = block_route[:, 0].astype(jnp.int32)
    row_rank = lax.map(rank_rows, flat_route.reshape(DEVICES, ROWS_DEV)).reshape(-1)
    device = jnp.arange(NROWS, dtype=jnp.int32) // ROWS_DEV
    vis_index = device // N_TILE
    tile_index = device % N_TILE
    block_id = ((flat_route // BLK_DEV) * N_TILE + tile_index) * BLK_DEV + flat_route % BLK_DEV
    slot_id = vis_index * CAP + row_rank
    slot_table = jnp.full((NBLK, N_VIS * CAP), -1, jnp.int32).at[block_id, slot_id].set(jnp.arange(NROWS, dtype=jnp.int32))
    table_u = w_plane * OS + u_frac
    table_v = w_plane * OS + v_frac
    codes_all = jnp.stack([u_cell.T, v_cell.T, table_u.T, table_v.T], axis=1).astype(jnp.int32)

    def grid_one(slot_rows):
        is_live = slot_rows >= 0
        safe_rows = jnp.maximum(slot_rows, 0)
        samples = jnp.where(is_live[:, None], vis_data[safe_rows], jnp.zeros((), jnp.bfloat16))
        samples = samples.reshape(-1, POLC)
        code_rows = jnp.transpose(codes_all[safe_rows], (1, 0, 2)).reshape(4, -1)
        return grid_block(samples, code_rows, kernel_taps, taper_gain)

    subgrids = lax.map(grid_one, slot_table)
    canvas = jnp.zeros((GT, TS, TS * POLC), jnp.float32)
    return place_tiles(canvas, subgrids, sub_tile[:, 0].astype(jnp.int32), sub_anchor, 0)
```

```python
import functools

import jax
import jax.numpy as jnp
from jax import lax
from jax.experimental import pallas as pl
from jax.experimental.pallas import tpu as pltpu
from jax.sharding import PartitionSpec as P

BLK_DEV = 8
SUB = 32
POLC = 8
TAPS = 7
OS = 16
TS = 256
GT = 8
SCAP = 2
LANES = 128
ROWS = 8
FAR = 1 << 20
NT = (((1,), (1,)), ((), ()))


def dispatch_kernel(
    slot_cap, vis, u_cell, v_cell, u_frac, v_frac, w_plane, route, out, feat, dest
):
    rows = vis.shape[0]
    columns = vis.shape[1]
    channels = u_cell.shape[0]
    owners, _, chunk = out.shape
    groups = owners * BLK_DEV
    feat[pl.ds(0, columns), :] = vis[...].astype(jnp.float32).T.astype(jnp.bfloat16)
    plane = w_plane[...] * OS
    codes = (u_cell[...], v_cell[...], plane + u_frac[...], plane + v_frac[...])
    for place, code in enumerate(codes):
        feat[pl.ds(columns + place * channels, channels), :] = code.astype(jnp.float32).astype(
            jnp.bfloat16
        )
    names = route[...]
    mine = lax.broadcasted_iota(jnp.int32, (groups, rows), 0) == names
    onehot = jnp.where(mine, 1.0, 0.0)
    earlier = lax.broadcasted_iota(jnp.int32, (rows, rows), 0) < lax.broadcasted_iota(
        jnp.int32, (rows, rows), 1
    )
    before = jnp.dot(
        onehot.astype(jnp.bfloat16),
        jnp.where(earlier, 1.0, 0.0).astype(jnp.bfloat16),
        preferred_element_type=jnp.float32,
    )
    rank = jnp.sum(onehot * before, axis=0, keepdims=True).astype(jnp.int32)
    dest[...] = names * slot_cap + rank

    def send(owner, _):
        slots = lax.broadcasted_iota(jnp.int32, (chunk, rows), 0) + owner * chunk
        pick = jnp.where(slots == dest[...], 1.0, 0.0).astype(jnp.bfloat16)
        out[owner] = lax.dot_general(
            feat[...], pick, NT, preferred_element_type=jnp.float32
        ).astype(jnp.bfloat16)
        return 0

    lax.fori_loop(0, owners, send, 0)


def spread(cell, taps, offsets):
    delta = offsets - cell
    weight = jnp.zeros(delta.shape, jnp.float32)
    for tap in range(TAPS):
        weight = jnp.where(delta == tap, taps[tap : tap + 1, :], weight)
    return weight


def grid_kernel(slot_cap, chunk, channels, slot_of, feat, table, taper, out, total, left, right):
    step = pl.program_id(0)
    covered = min(BLK_DEV, LANES // slot_cap)
    first = (step * LANES) % chunk // slot_cap
    columns = channels * POLC

    @pl.when(step == 0)
    def _():
        total[...] = jnp.zeros_like(total)
        out[...] = jnp.zeros_like(out)

    lanes = lax.broadcasted_iota(jnp.int32, (SUB, LANES), 1)
    block = (step * LANES + lanes) % chunk // slot_cap - first
    offsets = lax.broadcasted_iota(jnp.int32, (SUB, LANES), 0)
    samples = feat[0, pl.ds(0, columns), :].astype(jnp.float32)
    codes = feat[0, pl.ds(columns, 4 * channels), :].astype(jnp.float32).astype(jnp.int32)
    lookup = table[...]
    for h in range(channels):
        sample = samples[h * POLC : (h + 1) * POLC, :]
        cell_u = codes[h : h + 1, :]
        cell_v = codes[channels + h : channels + h + 1, :]
        row_u = codes[2 * channels + h : 2 * channels + h + 1, :]
        row_v = codes[3 * channels + h : 3 * channels + h + 1, :]
        taps_u = jnp.take_along_axis(lookup, jnp.broadcast_to(row_u, (8, LANES)), axis=1)
        taps_v = jnp.take_along_axis(lookup, jnp.broadcast_to(row_v, (8, LANES)), axis=1)
        weight_u = spread(cell_u, taps_u, offsets)
        weight_v = spread(cell_v, taps_v, offsets)
        here = pl.ds(h * LANES, LANES)
        weighted = weight_u[:, None, :] * sample[None, :, :]
        right[:, here] = weighted.reshape(SUB * POLC, LANES).astype(jnp.bfloat16)
        for b in range(covered):
            left[pl.ds(b * SUB, SUB), here] = jnp.where(block == b, weight_v, 0.0).astype(
                jnp.bfloat16
            )
    part = lax.dot_general(left[...], right[...], NT, preferred_element_type=jnp.float32)
    place = pl.ds(pl.multiple_of(first * SUB, SUB), covered * SUB)
    total[place, :] = total[place, :] + part

    @pl.when(step == pl.num_programs(0) - 1)
    def _():
        for b in range(BLK_DEV):
            sub = total[pl.ds(b * SUB, SUB), :] * taper[...]
            out[slot_of[b]] = sub.astype(jnp.bfloat16)


def place_kernel(tile_slots, offset_v, offset_u, subs, out, canvas):
    step = pl.program_id(0)
    slots = subs.shape[1]
    height = out.shape[1]
    width = out.shape[2]
    span = SUB * POLC

    @pl.when(step == 0)
    def _():
        canvas[...] = jnp.zeros_like(canvas)

    def add_one(slot, _):
        low = offset_v[step * slots + slot]
        column = offset_u[step * slots + slot]

        @pl.when((low > 0) & (low < height + SUB))
        def _():
            sub = subs[0, slot].astype(jnp.float32)
            sub = jnp.concatenate([sub, jnp.zeros((SUB, LANES), jnp.float32)], axis=1)
            sub = pltpu.roll(sub, column % LANES, 1)
            sub = jnp.concatenate([sub, jnp.zeros((ROWS, span + LANES), jnp.float32)], axis=0)
            sub = pltpu.roll(sub, low % ROWS, 0)
            top = pl.multiple_of(low // ROWS * ROWS, ROWS)
            base = pl.multiple_of(column // LANES * LANES, LANES)
            tile = slot % tile_slots // SCAP
            here = (tile, pl.ds(top, SUB + ROWS), pl.ds(base, span + LANES))
            canvas[here] = canvas[here] + sub

        return 0

    lax.fori_loop(0, slots, add_one, 0)

    @pl.when(step == pl.num_programs(0) - 1)
    def _():
        out[...] = canvas[:, pl.ds(SUB, height), pl.ds(0, width)]


def on_device(
    vis_data,
    u_cell,
    v_cell,
    u_frac,
    v_frac,
    w_plane,
    block_route,
    kernel_taps,
    taper_gain,
    sub_tile,
    sub_anchor,
):
    vis_count = lax.axis_size("vis")
    tile_width = lax.axis_size("tile")
    gt_dev = GT // tile_width
    rows, columns = vis_data.shape
    channels = u_cell.shape[0]
    slot_cap = max(2, 2 * rows // (BLK_DEV * vis_count))
    chunk = BLK_DEV * slot_cap
    features = columns + 4 * channels
    per_owner = gt_dev * SCAP
    slots = tile_width * per_owner
    height = TS // vis_count
    width = TS * POLC

    meta = jnp.concatenate([sub_tile, sub_anchor], axis=1)
    meta = lax.all_gather(meta, ("vis", "tile"), axis=0, tiled=True)
    meta = meta.reshape(vis_count * tile_width, BLK_DEV, 3)
    order = jnp.arange(BLK_DEV, dtype=jnp.int32)

    def ranks(tiles):
        same = tiles[..., :, None] == tiles[..., None, :]
        return jnp.sum((same & (order[None, :] < order[:, None])).astype(jnp.int32), axis=-1)

    wanted = jnp.arange(per_owner, dtype=jnp.int32)
    tiles_all = meta[:, :, 0]
    slot_all = (tiles_all - lax.axis_index("tile") * gt_dev) * SCAP + ranks(tiles_all)
    hit = slot_all[:, None, :] == wanted[None, :, None]
    low = jnp.sum(jnp.where(hit, meta[:, None, :, 1] + FAR, 0), axis=-1) - FAR
    offset_v = (low - lax.axis_index("vis") * height + SUB).reshape(-1)
    offset_u = jnp.sum(jnp.where(hit, meta[:, None, :, 2], 0), axis=-1).reshape(-1) * POLC

    send = pl.pallas_call(
        functools.partial(dispatch_kernel, slot_cap),
        out_shape=jax.ShapeDtypeStruct((vis_count, features, chunk), jnp.bfloat16),
        scratch_shapes=[
            pltpu.VMEM((features, rows), jnp.bfloat16),
            pltpu.VMEM((1, rows), jnp.int32),
        ],
        name="dispatch",
    )(vis_data, u_cell, v_cell, u_frac, v_frac, w_plane, block_route.reshape(1, rows))
    moved = lax.all_to_all(send, "vis", split_axis=0, concat_axis=0, tiled=True)
    if chunk % LANES:
        moved = jnp.transpose(moved, (1, 0, 2)).reshape(1, features, vis_count * chunk)
    per_source = moved.shape[2] // LANES
    steps = moved.shape[0] * per_source
    covered = min(BLK_DEV, LANES // slot_cap)

    table = jnp.pad(kernel_taps.astype(jnp.bfloat16).astype(jnp.float32).T, ((0, 8 - TAPS), (0, 0)))
    taper = jnp.repeat(taper_gain, POLC, axis=1)
    tile_ids = sub_tile[:, 0]
    slot_of = tile_ids * SCAP + ranks(tile_ids)
    subs = pl.pallas_call(
        functools.partial(grid_kernel, slot_cap, chunk, channels),
        grid_spec=pltpu.PrefetchScalarGridSpec(
            num_scalar_prefetch=1,
            grid=(steps,),
            in_specs=[
                pl.BlockSpec(
                    (1, features, LANES), lambda s, *_: (s // per_source, 0, s % per_source)
                ),
                pl.BlockSpec(table.shape, lambda s, *_: (0, 0)),
                pl.BlockSpec(taper.shape, lambda s, *_: (0, 0)),
            ],
            out_specs=pl.BlockSpec((slots, SUB, SUB * POLC), lambda s, *_: (0, 0, 0)),
            scratch_shapes=[
                pltpu.VMEM((BLK_DEV * SUB, SUB * POLC), jnp.float32),
                pltpu.VMEM((covered * SUB, channels * LANES), jnp.bfloat16),
                pltpu.VMEM((SUB * POLC, channels * LANES), jnp.bfloat16),
            ],
        ),
        out_shape=jax.ShapeDtypeStruct((slots, SUB, SUB * POLC), jnp.bfloat16),
        name="grid",
    )(slot_of, moved, table, taper)
    subs = lax.all_to_all(subs, "tile", split_axis=0, concat_axis=0, tiled=True)
    subs = lax.all_gather(subs, "vis", axis=0)
    return pl.pallas_call(
        functools.partial(place_kernel, per_owner),
        grid_spec=pltpu.PrefetchScalarGridSpec(
            num_scalar_prefetch=2,
            grid=(vis_count,),
            in_specs=[pl.BlockSpec((1, slots, SUB, SUB * POLC), lambda s, *_: (s, 0, 0, 0))],
            out_specs=pl.BlockSpec((gt_dev, height, width), lambda s, *_: (0, 0, 0)),
            scratch_shapes=[
                pltpu.VMEM((gt_dev, -(-height // ROWS) * ROWS + 2 * SUB + ROWS, width + LANES), jnp.float32),
            ],
        ),
        out_shape=jax.ShapeDtypeStruct((gt_dev, height, width), jnp.float32),
        name="place",
    )(offset_v, offset_u, subs)


def solution(mesh):
    placed = (
        P(("vis", "tile"), None),
        P(None, ("vis", "tile")),
        P(None, ("vis", "tile")),
        P(None, ("vis", "tile")),
        P(None, ("vis", "tile")),
        P(None, ("vis", "tile")),
        P(("vis", "tile"), None),
        P(),
        P(),
        P(("vis", "tile"), None),
        P(("vis", "tile"), None),
    )
    return jax.shard_map(
        on_device, mesh=mesh, in_specs=placed, out_specs=P("tile", "vis", None), check_vma=False
    )
```

```python
import functools

import jax
import jax.numpy as jnp
from jax import lax
from jax.experimental import pallas as pl
from jax.experimental.pallas import tpu as pltpu
from jax.sharding import PartitionSpec as P

BLK_DEV = 8
SUB = 32
POLC = 8
TAPS = 7
OS = 16
TS = 256
GT = 8
SCAP = 2
LANES = 128
ROWS = 8
FAR = 1 << 20
MESH = pl.DeviceIdType.MESH
NT = (((1,), (1,)), ((), ()))


def dispatch_kernel(
    slot_cap, vis, u_cell, v_cell, u_frac, v_frac, w_plane, route, out, feat, dest
):
    rows = vis.shape[0]
    columns = vis.shape[1]
    channels = u_cell.shape[0]
    owners, _, chunk = out.shape
    groups = owners * BLK_DEV
    feat[pl.ds(0, columns), :] = vis[...].astype(jnp.float32).T.astype(jnp.bfloat16)
    plane = w_plane[...] * OS
    codes = (u_cell[...], v_cell[...], plane + u_frac[...], plane + v_frac[...])
    for place, code in enumerate(codes):
        feat[pl.ds(columns + place * channels, channels), :] = code.astype(jnp.float32).astype(
            jnp.bfloat16
        )
    names = route[...]
    mine = lax.broadcasted_iota(jnp.int32, (groups, rows), 0) == names
    onehot = jnp.where(mine, 1.0, 0.0)
    earlier = lax.broadcasted_iota(jnp.int32, (rows, rows), 0) < lax.broadcasted_iota(
        jnp.int32, (rows, rows), 1
    )
    before = jnp.dot(
        onehot.astype(jnp.bfloat16),
        jnp.where(earlier, 1.0, 0.0).astype(jnp.bfloat16),
        preferred_element_type=jnp.float32,
    )
    rank = jnp.sum(onehot * before, axis=0, keepdims=True).astype(jnp.int32)
    dest[...] = names * slot_cap + rank

    def send(owner, _):
        slots = lax.broadcasted_iota(jnp.int32, (chunk, rows), 0) + owner * chunk
        pick = jnp.where(slots == dest[...], 1.0, 0.0).astype(jnp.bfloat16)
        out[owner] = lax.dot_general(
            feat[...], pick, NT, preferred_element_type=jnp.float32
        ).astype(jnp.bfloat16)
        return 0

    lax.fori_loop(0, owners, send, 0)


def spread(cell, taps, offsets):
    delta = offsets - cell
    weight = jnp.zeros(delta.shape, jnp.float32)
    for tap in range(TAPS):
        weight = jnp.where(delta == tap, taps[tap : tap + 1, :], weight)
    return weight


def grid_kernel(slot_cap, chunk, channels, slot_of, feat, table, taper, out, total, left, right):
    step = pl.program_id(0)
    covered = min(BLK_DEV, LANES // slot_cap)
    first = (step * LANES) % chunk // slot_cap
    columns = channels * POLC

    @pl.when(step == 0)
    def _():
        total[...] = jnp.zeros_like(total)
        out[...] = jnp.zeros_like(out)

    lanes = lax.broadcasted_iota(jnp.int32, (SUB, LANES), 1)
    block = (step * LANES + lanes) % chunk // slot_cap - first
    offsets = lax.broadcasted_iota(jnp.int32, (SUB, LANES), 0)
    samples = feat[0, pl.ds(0, columns), :].astype(jnp.float32)
    codes = feat[0, pl.ds(columns, 4 * channels), :].astype(jnp.float32).astype(jnp.int32)
    lookup = table[...]
    for h in range(channels):
        sample = samples[h * POLC : (h + 1) * POLC, :]
        cell_u = codes[h : h + 1, :]
        cell_v = codes[channels + h : channels + h + 1, :]
        row_u = codes[2 * channels + h : 2 * channels + h + 1, :]
        row_v = codes[3 * channels + h : 3 * channels + h + 1, :]
        taps_u = jnp.take_along_axis(lookup, jnp.broadcast_to(row_u, (8, LANES)), axis=1)
        taps_v = jnp.take_along_axis(lookup, jnp.broadcast_to(row_v, (8, LANES)), axis=1)
        weight_u = spread(cell_u, taps_u, offsets)
        weight_v = spread(cell_v, taps_v, offsets)
        here = pl.ds(h * LANES, LANES)
        weighted = weight_u[:, None, :] * sample[None, :, :]
        right[:, here] = weighted.reshape(SUB * POLC, LANES).astype(jnp.bfloat16)
        for b in range(covered):
            left[pl.ds(b * SUB, SUB), here] = jnp.where(block == b, weight_v, 0.0).astype(
                jnp.bfloat16
            )
    part = lax.dot_general(left[...], right[...], NT, preferred_element_type=jnp.float32)
    place = pl.ds(pl.multiple_of(first * SUB, SUB), covered * SUB)
    total[place, :] = total[place, :] + part

    @pl.when(step == pl.num_programs(0) - 1)
    def _():
        for b in range(BLK_DEV):
            sub = total[pl.ds(b * SUB, SUB), :] * taper[...]
            out[slot_of[b]] = sub.astype(jnp.bfloat16)


def gather_kernel(subs, meta, out, meta_out, own_sem, near_send, near_recv, far_send, far_recv):
    count = out.shape[0]
    width = out.shape[1]
    v, t = lax.axis_index("vis"), lax.axis_index("tile")
    half = count // 2
    spot = v // 2 * (1 - v % 2) + (count - 1 - v // 2) * (v % 2)

    def member(position):
        position = (position + 2 * count) % count
        back = position // half
        return (1 - back) * 2 * position + back * (2 * (count - 1 - position) + 1)

    barrier = pltpu.get_barrier_semaphore()
    for side in (1, -1):
        pl.semaphore_signal(
            barrier, inc=1, device_id=(member(spot + side), t), device_id_type=MESH
        )
    for k in range(1, width):
        pl.semaphore_signal(barrier, inc=1, device_id=(v, (t + k) % width), device_id_type=MESH)
    pl.semaphore_wait(barrier, 1 + width)

    def near(k):
        chunk = pl.ds((t + k) % width, 1)
        pairs = ((subs.at[chunk], out.at[v, pl.ds(t, 1)]), (meta, meta_out.at[v, t]))
        return [
            pltpu.make_async_remote_copy(
                src_ref=src,
                dst_ref=dst,
                send_sem=near_send.at[2 * k + i],
                recv_sem=near_recv.at[2 * k + i],
                device_id=(v, (t + k) % width),
                device_id_type=MESH,
            )
            for i, (src, dst) in enumerate(pairs)
        ]

    def own():
        pairs = ((subs.at[pl.ds(t, 1)], out.at[v, pl.ds(t, 1)]), (meta, meta_out.at[v, t]))
        return [
            pltpu.make_async_copy(src, dst, own_sem.at[i]) for i, (src, dst) in enumerate(pairs)
        ]

    def far(k, step):
        side = 1 - 2 * (k % 2)
        origin = member(spot - side * step)
        source = (t + width - k) % width
        refs = (out.at[origin, pl.ds(source, 1)], meta_out.at[origin, source])
        return [
            pltpu.make_async_remote_copy(
                src_ref=ref,
                dst_ref=ref,
                send_sem=far_send.at[(step * width + k) * 2 + i],
                recv_sem=far_recv.at[(step * width + k) * 2 + i],
                device_id=(member(spot + side), t),
                device_id_type=MESH,
            )
            for i, ref in enumerate(refs)
        ]

    for copy in own():
        copy.start()
    for k in range(1, width):
        for copy in near(k):
            copy.start()
    for copy in own():
        copy.wait()
    for k in range(width):
        if k:
            for copy in near(k):
                copy.wait_recv()
        for copy in far(k, 0):
            copy.start()

    def forward(step, _):
        for k in range(width):
            for copy in far(k, step - 1):
                copy.wait_recv()
            for copy in far(k, step):
                copy.start()
        return 0

    lax.fori_loop(1, count - 1, forward, 0)
    for k in range(width):
        for copy in far(k, count - 2):
            copy.wait_recv()
    for k in range(1, width):
        for copy in near(k):
            copy.wait_send()

    def sent(step, _):
        for k in range(width):
            for copy in far(k, step):
                copy.wait_send()
        return 0

    lax.fori_loop(0, count - 1, sent, 0)


def place_kernel(tile_slots, offset_v, offset_u, subs, out, canvas):
    step = pl.program_id(0)
    slots = subs.shape[1]
    height = out.shape[1]
    width = out.shape[2]
    span = SUB * POLC

    @pl.when(step == 0)
    def _():
        canvas[...] = jnp.zeros_like(canvas)

    def add_one(slot, _):
        low = offset_v[step * slots + slot]
        column = offset_u[step * slots + slot]

        @pl.when((low > 0) & (low < height + SUB))
        def _():
            sub = subs[0, slot].astype(jnp.float32)
            sub = jnp.concatenate([sub, jnp.zeros((SUB, LANES), jnp.float32)], axis=1)
            sub = pltpu.roll(sub, column % LANES, 1)
            sub = jnp.concatenate([sub, jnp.zeros((ROWS, span + LANES), jnp.float32)], axis=0)
            sub = pltpu.roll(sub, low % ROWS, 0)
            top = pl.multiple_of(low // ROWS * ROWS, ROWS)
            base = pl.multiple_of(column // LANES * LANES, LANES)
            tile = slot % tile_slots // SCAP
            here = (tile, pl.ds(top, SUB + ROWS), pl.ds(base, span + LANES))
            canvas[here] = canvas[here] + sub

        return 0

    lax.fori_loop(0, slots, add_one, 0)

    @pl.when(step == pl.num_programs(0) - 1)
    def _():
        out[...] = canvas[:, pl.ds(SUB, height), pl.ds(0, width)]


def on_device(
    vis_data,
    u_cell,
    v_cell,
    u_frac,
    v_frac,
    w_plane,
    block_route,
    kernel_taps,
    taper_gain,
    sub_tile,
    sub_anchor,
):
    vis_count = lax.axis_size("vis")
    tile_width = lax.axis_size("tile")
    gt_dev = GT // tile_width
    rows, columns = vis_data.shape
    channels = u_cell.shape[0]
    slot_cap = max(2, 2 * rows // (BLK_DEV * vis_count))
    chunk = BLK_DEV * slot_cap
    features = columns + 4 * channels
    per_owner = gt_dev * SCAP
    slots = tile_width * per_owner
    height = TS // vis_count
    width = TS * POLC

    order = jnp.arange(BLK_DEV, dtype=jnp.int32)

    def ranks(tiles):
        same = tiles[..., :, None] == tiles[..., None, :]
        return jnp.sum((same & (order[None, :] < order[:, None])).astype(jnp.int32), axis=-1)

    send = pl.pallas_call(
        functools.partial(dispatch_kernel, slot_cap),
        out_shape=jax.ShapeDtypeStruct((vis_count, features, chunk), jnp.bfloat16),
        scratch_shapes=[
            pltpu.VMEM((features, rows), jnp.bfloat16),
            pltpu.VMEM((1, rows), jnp.int32),
        ],
        name="dispatch",
    )(vis_data, u_cell, v_cell, u_frac, v_frac, w_plane, block_route.reshape(1, rows))
    moved = lax.all_to_all(send, "vis", split_axis=0, concat_axis=0, tiled=True)
    if chunk % LANES:
        moved = jnp.transpose(moved, (1, 0, 2)).reshape(1, features, vis_count * chunk)
    per_source = moved.shape[2] // LANES
    steps = moved.shape[0] * per_source
    covered = min(BLK_DEV, LANES // slot_cap)

    table = jnp.pad(kernel_taps.astype(jnp.bfloat16).astype(jnp.float32).T, ((0, 8 - TAPS), (0, 0)))
    taper = jnp.repeat(taper_gain, POLC, axis=1)
    tile_ids = sub_tile[:, 0]
    slot_of = tile_ids * SCAP + ranks(tile_ids)
    subs = pl.pallas_call(
        functools.partial(grid_kernel, slot_cap, chunk, channels),
        grid_spec=pltpu.PrefetchScalarGridSpec(
            num_scalar_prefetch=1,
            grid=(steps,),
            in_specs=[
                pl.BlockSpec(
                    (1, features, LANES), lambda s, *_: (s // per_source, 0, s % per_source)
                ),
                pl.BlockSpec(table.shape, lambda s, *_: (0, 0)),
                pl.BlockSpec(taper.shape, lambda s, *_: (0, 0)),
            ],
            out_specs=pl.BlockSpec((slots, SUB, SUB * POLC), lambda s, *_: (0, 0, 0)),
            scratch_shapes=[
                pltpu.VMEM((BLK_DEV * SUB, SUB * POLC), jnp.float32),
                pltpu.VMEM((covered * SUB, channels * LANES), jnp.bfloat16),
                pltpu.VMEM((SUB * POLC, channels * LANES), jnp.bfloat16),
            ],
        ),
        out_shape=jax.ShapeDtypeStruct((slots, SUB, SUB * POLC), jnp.bfloat16),
        name="grid",
    )(slot_of, moved, table, taper)
    meta = jnp.concatenate([tile_ids, sub_anchor[:, 0], sub_anchor[:, 1]])
    meta = jnp.pad(meta, (0, LANES - meta.shape[0])).reshape(1, LANES)
    hops = (vis_count - 1) * tile_width * 2
    vmem = pl.BlockSpec(memory_space=pltpu.VMEM)
    subs, meta = pl.pallas_call(
        gather_kernel,
        in_specs=[vmem, vmem],
        out_specs=[vmem, vmem],
        out_shape=[
            jax.ShapeDtypeStruct(
                (vis_count, tile_width, per_owner, SUB, SUB * POLC), jnp.bfloat16
            ),
            jax.ShapeDtypeStruct((vis_count, tile_width, 1, LANES), jnp.int32),
        ],
        scratch_shapes=[
            pltpu.SemaphoreType.DMA((2,)),
            pltpu.SemaphoreType.DMA((2 * tile_width,)),
            pltpu.SemaphoreType.DMA((2 * tile_width,)),
            pltpu.SemaphoreType.DMA((hops,)),
            pltpu.SemaphoreType.DMA((hops,)),
        ],
        compiler_params=pltpu.CompilerParams(collective_id=0, has_side_effects=True),
        name="gather",
    )(subs.reshape(tile_width, per_owner, SUB, SUB * POLC), meta)
    subs = subs.reshape(vis_count, slots, SUB, SUB * POLC)
    meta = meta.reshape(vis_count * tile_width, LANES)[:, : 3 * BLK_DEV]
    meta = meta.reshape(vis_count * tile_width, 3, BLK_DEV)

    wanted = jnp.arange(per_owner, dtype=jnp.int32)
    tiles_all = meta[:, 0]
    slot_all = (tiles_all - lax.axis_index("tile") * gt_dev) * SCAP + ranks(tiles_all)
    hit = slot_all[:, None, :] == wanted[None, :, None]
    low = jnp.sum(jnp.where(hit, meta[:, 1][:, None] + FAR, 0), axis=-1) - FAR
    offset_v = (low - lax.axis_index("vis") * height + SUB).reshape(-1)
    offset_u = jnp.sum(jnp.where(hit, meta[:, 2][:, None], 0), axis=-1).reshape(-1) * POLC
    return pl.pallas_call(
        functools.partial(place_kernel, per_owner),
        grid_spec=pltpu.PrefetchScalarGridSpec(
            num_scalar_prefetch=2,
            grid=(vis_count,),
            in_specs=[pl.BlockSpec((1, slots, SUB, SUB * POLC), lambda s, *_: (s, 0, 0, 0))],
            out_specs=pl.BlockSpec((gt_dev, height, width), lambda s, *_: (0, 0, 0)),
            scratch_shapes=[
                pltpu.VMEM((gt_dev, -(-height // ROWS) * ROWS + 2 * SUB + ROWS, width + LANES), jnp.float32),
            ],
        ),
        out_shape=jax.ShapeDtypeStruct((gt_dev, height, width), jnp.float32),
        name="place",
    )(offset_v, offset_u, subs)


def solution(mesh):
    placed = (
        P(("vis", "tile"), None),
        P(None, ("vis", "tile")),
        P(None, ("vis", "tile")),
        P(None, ("vis", "tile")),
        P(None, ("vis", "tile")),
        P(None, ("vis", "tile")),
        P(("vis", "tile"), None),
        P(),
        P(),
        P(("vis", "tile"), None),
        P(("vis", "tile"), None),
    )
    return jax.shard_map(
        on_device, mesh=mesh, in_specs=placed, out_specs=P("tile", "vis", None), check_vma=False
    )
```

```python
import functools

import jax
import jax.numpy as jnp
from jax import lax
from jax.experimental import pallas as pl
from jax.experimental.pallas import tpu as pltpu
from jax.sharding import PartitionSpec as P

BLK_DEV = 8
SUB = 32
POLC = 8
TAPS = 7
OS = 16
TS = 256
GT = 8
SCAP = 2
LANES = 128
ROWS = 8
FAR = 1 << 20
MESH = pl.DeviceIdType.MESH
NT = (((1,), (1,)), ((), ()))


def dispatch_kernel(
    slot_cap, vis, u_cell, v_cell, u_frac, v_frac, w_plane, route, out, feat, dest
):
    rows = vis.shape[0]
    columns = vis.shape[1]
    channels = u_cell.shape[0]
    owners, _, chunk = out.shape
    groups = owners * BLK_DEV
    feat[pl.ds(0, columns), :] = vis[...].astype(jnp.float32).T.astype(jnp.bfloat16)
    plane = w_plane[...] * OS
    codes = (u_cell[...], v_cell[...], plane + u_frac[...], plane + v_frac[...])
    for place, code in enumerate(codes):
        feat[pl.ds(columns + place * channels, channels), :] = code.astype(jnp.float32).astype(
            jnp.bfloat16
        )
    names = route[...]
    mine = lax.broadcasted_iota(jnp.int32, (groups, rows), 0) == names
    onehot = jnp.where(mine, 1.0, 0.0)
    earlier = lax.broadcasted_iota(jnp.int32, (rows, rows), 0) < lax.broadcasted_iota(
        jnp.int32, (rows, rows), 1
    )
    before = jnp.dot(
        onehot.astype(jnp.bfloat16),
        jnp.where(earlier, 1.0, 0.0).astype(jnp.bfloat16),
        preferred_element_type=jnp.float32,
    )
    rank = jnp.sum(onehot * before, axis=0, keepdims=True).astype(jnp.int32)
    dest[...] = names * slot_cap + rank

    def send(owner, _):
        slots = lax.broadcasted_iota(jnp.int32, (chunk, rows), 0) + owner * chunk
        pick = jnp.where(slots == dest[...], 1.0, 0.0).astype(jnp.bfloat16)
        out[owner] = lax.dot_general(
            feat[...], pick, NT, preferred_element_type=jnp.float32
        ).astype(jnp.bfloat16)
        return 0

    lax.fori_loop(0, owners, send, 0)


def spread(cell, taps, offsets):
    delta = offsets - cell
    weight = jnp.zeros(delta.shape, jnp.float32)
    for tap in range(TAPS):
        weight = jnp.where(delta == tap, taps[tap : tap + 1, :], weight)
    return weight


def grid_chunk(slot_cap, chunk, channels, lane, feat, table, total, left, right):
    covered = min(BLK_DEV, LANES // slot_cap)
    first = lane % chunk // slot_cap
    columns = channels * POLC
    lanes = lax.broadcasted_iota(jnp.int32, (SUB, LANES), 1)
    block = (lane + lanes) % chunk // slot_cap - first
    offsets = lax.broadcasted_iota(jnp.int32, (SUB, LANES), 0)
    samples = feat[:columns, :].astype(jnp.float32)
    codes = feat[columns:, :].astype(jnp.float32).astype(jnp.int32)
    lookup = table[...]
    for h in range(channels):
        sample = samples[h * POLC : (h + 1) * POLC, :]
        cell_u = codes[h : h + 1, :]
        cell_v = codes[channels + h : channels + h + 1, :]
        row_u = codes[2 * channels + h : 2 * channels + h + 1, :]
        row_v = codes[3 * channels + h : 3 * channels + h + 1, :]
        taps_u = jnp.take_along_axis(lookup, jnp.broadcast_to(row_u, (8, LANES)), axis=1)
        taps_v = jnp.take_along_axis(lookup, jnp.broadcast_to(row_v, (8, LANES)), axis=1)
        weight_u = spread(cell_u, taps_u, offsets)
        weight_v = spread(cell_v, taps_v, offsets)
        here = pl.ds(h * LANES, LANES)
        weighted = weight_u[:, None, :] * sample[None, :, :]
        right[:, here] = weighted.reshape(SUB * POLC, LANES).astype(jnp.bfloat16)
        for b in range(covered):
            left[pl.ds(b * SUB, SUB), here] = jnp.where(block == b, weight_v, 0.0).astype(
                jnp.bfloat16
            )
    part = lax.dot_general(left[...], right[...], NT, preferred_element_type=jnp.float32)
    place = pl.ds(pl.multiple_of(first * SUB, SUB), covered * SUB)
    total[place, :] = total[place, :] + part


def grid_kernel(slot_cap, chunk, channels, feat, table, taper, out, total, left, right):
    step = pl.program_id(0)

    @pl.when(step == 0)
    def _():
        total[...] = jnp.zeros_like(total)

    grid_chunk(
        slot_cap, chunk, channels, step * LANES, feat[0], table, total, left, right
    )

    @pl.when(step == pl.num_programs(0) - 1)
    def _():
        for b in range(BLK_DEV):
            out[b] = (total[pl.ds(b * SUB, SUB), :] * taper[...]).astype(jnp.bfloat16)


def move_grid_kernel(
    slot_cap, channels, send, table, taper, out, moved, total, left, right, own_sem, to_sem, at_sem
):
    count, features, chunk = send.shape
    v, t = lax.axis_index("vis"), lax.axis_index("tile")
    barrier = pltpu.get_barrier_semaphore()
    for k in range(1, count):
        pl.semaphore_signal(barrier, inc=1, device_id=((v + k) % count, t), device_id_type=MESH)
    pl.semaphore_wait(barrier, count - 1)

    def copy(k):
        return pltpu.make_async_remote_copy(
            src_ref=send.at[(v + k) % count],
            dst_ref=moved.at[v],
            send_sem=to_sem.at[k],
            recv_sem=at_sem.at[k],
            device_id=((v + k) % count, t),
            device_id_type=MESH,
        )

    own = pltpu.make_async_copy(send.at[v], moved.at[v], own_sem.at[0])
    own.start()
    for k in range(1, count):
        copy(k).start()
    total[...] = jnp.zeros_like(total)
    own.wait()

    def source(k, _):
        @pl.when(k > 0)
        def _():
            copy(k).wait_recv()

        origin = (v + count - k) % count

        def part(piece, _):
            lane = pl.multiple_of(piece * LANES, LANES)
            grid_chunk(
                slot_cap,
                chunk,
                channels,
                lane,
                moved[origin, :, pl.ds(lane, LANES)],
                table,
                total,
                left,
                right,
            )
            return 0

        lax.fori_loop(0, chunk // LANES, part, 0)
        return 0

    lax.fori_loop(0, count, source, 0)
    for b in range(BLK_DEV):
        out[b] = (total[pl.ds(b * SUB, SUB), :] * taper[...]).astype(jnp.bfloat16)
    for k in range(1, count):
        copy(k).wait_send()


def slot_kernel(slot_of, subs, out):
    out[...] = jnp.zeros_like(out)
    for b in range(BLK_DEV):
        out[slot_of[b]] = subs[b]


def gather_kernel(subs, meta, out, meta_out, own_sem, near_send, near_recv, far_send, far_recv):
    count = out.shape[0]
    width = out.shape[1]
    v, t = lax.axis_index("vis"), lax.axis_index("tile")
    half = count // 2
    spot = v // 2 * (1 - v % 2) + (count - 1 - v // 2) * (v % 2)

    def member(position):
        position = (position + 2 * count) % count
        back = position // half
        return (1 - back) * 2 * position + back * (2 * (count - 1 - position) + 1)

    barrier = pltpu.get_barrier_semaphore()
    for side in (1, -1):
        pl.semaphore_signal(
            barrier, inc=1, device_id=(member(spot + side), t), device_id_type=MESH
        )
    for k in range(1, width):
        pl.semaphore_signal(barrier, inc=1, device_id=(v, (t + k) % width), device_id_type=MESH)
    pl.semaphore_wait(barrier, 1 + width)

    def near(k):
        chunk = pl.ds((t + k) % width, 1)
        pairs = ((subs.at[chunk], out.at[v, pl.ds(t, 1)]), (meta, meta_out.at[v, t]))
        return [
            pltpu.make_async_remote_copy(
                src_ref=src,
                dst_ref=dst,
                send_sem=near_send.at[2 * k + i],
                recv_sem=near_recv.at[2 * k + i],
                device_id=(v, (t + k) % width),
                device_id_type=MESH,
            )
            for i, (src, dst) in enumerate(pairs)
        ]

    def own():
        pairs = ((subs.at[pl.ds(t, 1)], out.at[v, pl.ds(t, 1)]), (meta, meta_out.at[v, t]))
        return [
            pltpu.make_async_copy(src, dst, own_sem.at[i]) for i, (src, dst) in enumerate(pairs)
        ]

    def far(k, step):
        side = 1 - 2 * (k % 2)
        origin = member(spot - side * step)
        source = (t + width - k) % width
        refs = (out.at[origin, pl.ds(source, 1)], meta_out.at[origin, source])
        return [
            pltpu.make_async_remote_copy(
                src_ref=ref,
                dst_ref=ref,
                send_sem=far_send.at[(step * width + k) * 2 + i],
                recv_sem=far_recv.at[(step * width + k) * 2 + i],
                device_id=(member(spot + side), t),
                device_id_type=MESH,
            )
            for i, ref in enumerate(refs)
        ]

    for copy in own():
        copy.start()
    for k in range(1, width):
        for copy in near(k):
            copy.start()
    for copy in own():
        copy.wait()
    for k in range(width):
        if k:
            for copy in near(k):
                copy.wait_recv()
        for copy in far(k, 0):
            copy.start()

    def forward(step, _):
        for k in range(width):
            for copy in far(k, step - 1):
                copy.wait_recv()
            for copy in far(k, step):
                copy.start()
        return 0

    lax.fori_loop(1, count - 1, forward, 0)
    for k in range(width):
        for copy in far(k, count - 2):
            copy.wait_recv()
    for k in range(1, width):
        for copy in near(k):
            copy.wait_send()

    def sent(step, _):
        for k in range(width):
            for copy in far(k, step):
                copy.wait_send()
        return 0

    lax.fori_loop(0, count - 1, sent, 0)


def place_kernel(tile_slots, offset_v, offset_u, subs, out, canvas):
    step = pl.program_id(0)
    slots = subs.shape[1]
    height = out.shape[1]
    width = out.shape[2]
    span = SUB * POLC

    @pl.when(step == 0)
    def _():
        canvas[...] = jnp.zeros_like(canvas)

    def add_one(slot, _):
        low = offset_v[step * slots + slot]
        column = offset_u[step * slots + slot]

        @pl.when((low > 0) & (low < height + SUB))
        def _():
            sub = subs[0, slot].astype(jnp.float32)
            sub = jnp.concatenate([sub, jnp.zeros((SUB, LANES), jnp.float32)], axis=1)
            sub = pltpu.roll(sub, column % LANES, 1)
            sub = jnp.concatenate([sub, jnp.zeros((ROWS, span + LANES), jnp.float32)], axis=0)
            sub = pltpu.roll(sub, low % ROWS, 0)
            top = pl.multiple_of(low // ROWS * ROWS, ROWS)
            base = pl.multiple_of(column // LANES * LANES, LANES)
            tile = slot % tile_slots // SCAP
            here = (tile, pl.ds(top, SUB + ROWS), pl.ds(base, span + LANES))
            canvas[here] = canvas[here] + sub

        return 0

    lax.fori_loop(0, slots, add_one, 0)

    @pl.when(step == pl.num_programs(0) - 1)
    def _():
        out[...] = canvas[:, pl.ds(SUB, height), pl.ds(0, width)]


def on_device(
    vis_data,
    u_cell,
    v_cell,
    u_frac,
    v_frac,
    w_plane,
    block_route,
    kernel_taps,
    taper_gain,
    sub_tile,
    sub_anchor,
):
    vis_count = lax.axis_size("vis")
    tile_width = lax.axis_size("tile")
    gt_dev = GT // tile_width
    rows, columns = vis_data.shape
    channels = u_cell.shape[0]
    slot_cap = max(2, 2 * rows // (BLK_DEV * vis_count))
    chunk = BLK_DEV * slot_cap
    features = columns + 4 * channels
    per_owner = gt_dev * SCAP
    slots = tile_width * per_owner
    height = TS // vis_count
    width = TS * POLC

    order = jnp.arange(BLK_DEV, dtype=jnp.int32)

    def ranks(tiles):
        same = tiles[..., :, None] == tiles[..., None, :]
        return jnp.sum((same & (order[None, :] < order[:, None])).astype(jnp.int32), axis=-1)

    send = pl.pallas_call(
        functools.partial(dispatch_kernel, slot_cap),
        out_shape=jax.ShapeDtypeStruct((vis_count, features, chunk), jnp.bfloat16),
        scratch_shapes=[
            pltpu.VMEM((features, rows), jnp.bfloat16),
            pltpu.VMEM((1, rows), jnp.int32),
        ],
        name="dispatch",
    )(vis_data, u_cell, v_cell, u_frac, v_frac, w_plane, block_route.reshape(1, rows))
    table = jnp.pad(kernel_taps.astype(jnp.bfloat16).astype(jnp.float32).T, ((0, 8 - TAPS), (0, 0)))
    taper = jnp.repeat(taper_gain, POLC, axis=1)
    covered = min(BLK_DEV, LANES // slot_cap)
    vmem = pl.BlockSpec(memory_space=pltpu.VMEM)
    work = [
        pltpu.VMEM((BLK_DEV * SUB, SUB * POLC), jnp.float32),
        pltpu.VMEM((covered * SUB, channels * LANES), jnp.bfloat16),
        pltpu.VMEM((SUB * POLC, channels * LANES), jnp.bfloat16),
    ]
    gridded = jax.ShapeDtypeStruct((BLK_DEV, SUB, SUB * POLC), jnp.bfloat16)
    if chunk % LANES == 0:
        subs = pl.pallas_call(
            functools.partial(move_grid_kernel, slot_cap, channels),
            in_specs=[vmem, vmem, vmem],
            out_specs=vmem,
            out_shape=gridded,
            scratch_shapes=[pltpu.VMEM(send.shape, jnp.bfloat16)]
            + work
            + [
                pltpu.SemaphoreType.DMA((1,)),
                pltpu.SemaphoreType.DMA((vis_count,)),
                pltpu.SemaphoreType.DMA((vis_count,)),
            ],
            compiler_params=pltpu.CompilerParams(collective_id=1, has_side_effects=True),
            name="move_grid",
        )(send, table, taper)
    else:
        moved = lax.all_to_all(send, "vis", split_axis=0, concat_axis=0, tiled=True)
        moved = jnp.transpose(moved, (1, 0, 2)).reshape(1, features, vis_count * chunk)
        subs = pl.pallas_call(
            functools.partial(grid_kernel, slot_cap, chunk, channels),
            grid=(moved.shape[2] // LANES,),
            in_specs=[
                pl.BlockSpec((1, features, LANES), lambda s: (0, 0, s)),
                pl.BlockSpec(table.shape, lambda s: (0, 0)),
                pl.BlockSpec(taper.shape, lambda s: (0, 0)),
            ],
            out_specs=pl.BlockSpec(gridded.shape, lambda s: (0, 0, 0)),
            out_shape=gridded,
            scratch_shapes=work,
            name="grid",
        )(moved, table, taper)
    tile_ids = sub_tile[:, 0]
    slot_of = tile_ids * SCAP + ranks(tile_ids)
    subs = pl.pallas_call(
        slot_kernel,
        in_specs=[pl.BlockSpec(memory_space=pltpu.SMEM), vmem],
        out_specs=vmem,
        out_shape=jax.ShapeDtypeStruct((slots, SUB, SUB * POLC), jnp.bfloat16),
        name="slot",
    )(slot_of, subs)
    meta = jnp.concatenate([tile_ids, sub_anchor[:, 0], sub_anchor[:, 1]])
    meta = jnp.pad(meta, (0, LANES - meta.shape[0])).reshape(1, LANES)
    hops = (vis_count - 1) * tile_width * 2
    subs, meta = pl.pallas_call(
        gather_kernel,
        in_specs=[vmem, vmem],
        out_specs=[vmem, vmem],
        out_shape=[
            jax.ShapeDtypeStruct(
                (vis_count, tile_width, per_owner, SUB, SUB * POLC), jnp.bfloat16
            ),
            jax.ShapeDtypeStruct((vis_count, tile_width, 1, LANES), jnp.int32),
        ],
        scratch_shapes=[
            pltpu.SemaphoreType.DMA((2,)),
            pltpu.SemaphoreType.DMA((2 * tile_width,)),
            pltpu.SemaphoreType.DMA((2 * tile_width,)),
            pltpu.SemaphoreType.DMA((hops,)),
            pltpu.SemaphoreType.DMA((hops,)),
        ],
        compiler_params=pltpu.CompilerParams(collective_id=0, has_side_effects=True),
        name="gather",
    )(subs.reshape(tile_width, per_owner, SUB, SUB * POLC), meta)
    subs = subs.reshape(vis_count, slots, SUB, SUB * POLC)
    meta = meta.reshape(vis_count * tile_width, LANES)[:, : 3 * BLK_DEV]
    meta = meta.reshape(vis_count * tile_width, 3, BLK_DEV)

    wanted = jnp.arange(per_owner, dtype=jnp.int32)
    tiles_all = meta[:, 0]
    slot_all = (tiles_all - lax.axis_index("tile") * gt_dev) * SCAP + ranks(tiles_all)
    hit = slot_all[:, None, :] == wanted[None, :, None]
    low = jnp.sum(jnp.where(hit, meta[:, 1][:, None] + FAR, 0), axis=-1) - FAR
    offset_v = (low - lax.axis_index("vis") * height + SUB).reshape(-1)
    offset_u = jnp.sum(jnp.where(hit, meta[:, 2][:, None], 0), axis=-1).reshape(-1) * POLC
    return pl.pallas_call(
        functools.partial(place_kernel, per_owner),
        grid_spec=pltpu.PrefetchScalarGridSpec(
            num_scalar_prefetch=2,
            grid=(vis_count,),
            in_specs=[pl.BlockSpec((1, slots, SUB, SUB * POLC), lambda s, *_: (s, 0, 0, 0))],
            out_specs=pl.BlockSpec((gt_dev, height, width), lambda s, *_: (0, 0, 0)),
            scratch_shapes=[
                pltpu.VMEM((gt_dev, -(-height // ROWS) * ROWS + 2 * SUB + ROWS, width + LANES), jnp.float32),
            ],
        ),
        out_shape=jax.ShapeDtypeStruct((gt_dev, height, width), jnp.float32),
        name="place",
    )(offset_v, offset_u, subs)


def solution(mesh):
    placed = (
        P(("vis", "tile"), None),
        P(None, ("vis", "tile")),
        P(None, ("vis", "tile")),
        P(None, ("vis", "tile")),
        P(None, ("vis", "tile")),
        P(None, ("vis", "tile")),
        P(("vis", "tile"), None),
        P(),
        P(),
        P(("vis", "tile"), None),
        P(("vis", "tile"), None),
    )
    return jax.shard_map(
        on_device, mesh=mesh, in_specs=placed, out_specs=P("tile", "vis", None), check_vma=False
    )
```

```python
import functools

import jax
import jax.numpy as jnp
from jax import lax
from jax.experimental import pallas as pl
from jax.experimental.pallas import tpu as pltpu
from jax.sharding import PartitionSpec as P

BLK_DEV = 8
SUB = 32
POLC = 8
TAPS = 7
OS = 16
TS = 256
GT = 8
SCAP = 2
LANES = 128
ROWS = 8
GROUP = 4
FAR = 1 << 20
MESH = pl.DeviceIdType.MESH
NT = (((1,), (1,)), ((), ()))


def dispatch_kernel(
    slot_cap, vis, u_cell, v_cell, u_frac, v_frac, w_plane, route, taps, gain, out, table, taper, feat, dest
):
    rows = vis.shape[0]
    columns = vis.shape[1]
    channels = u_cell.shape[0]
    owners, _, chunk = out.shape
    groups = owners * BLK_DEV
    feat[pl.ds(0, columns), :] = vis[...].astype(jnp.float32).T.astype(jnp.bfloat16)
    plane = w_plane[...] * OS
    codes = (u_cell[...], v_cell[...], plane + u_frac[...], plane + v_frac[...])
    for place, code in enumerate(codes):
        feat[pl.ds(columns + place * channels, channels), :] = code.astype(jnp.float32).astype(
            jnp.bfloat16
        )
    names = route[...]
    mine = lax.broadcasted_iota(jnp.int32, (groups, rows), 0) == names
    onehot = jnp.where(mine, 1.0, 0.0)
    earlier = lax.broadcasted_iota(jnp.int32, (rows, rows), 0) < lax.broadcasted_iota(
        jnp.int32, (rows, rows), 1
    )
    before = jnp.dot(
        onehot.astype(jnp.bfloat16),
        jnp.where(earlier, 1.0, 0.0).astype(jnp.bfloat16),
        preferred_element_type=jnp.float32,
    )
    rank = jnp.sum(onehot * before, axis=0, keepdims=True).astype(jnp.int32)
    dest[...] = names * slot_cap + rank

    turn = lax.broadcasted_iota(jnp.int32, (ROWS, TAPS), 0) == lax.broadcasted_iota(
        jnp.int32, (ROWS, TAPS), 1
    )
    table[...] = lax.dot_general(
        jnp.where(turn, 1.0, 0.0).astype(jnp.bfloat16),
        taps[...].astype(jnp.bfloat16),
        NT,
        preferred_element_type=jnp.float32,
    )
    cells = lax.broadcasted_iota(jnp.int32, (SUB, SUB * POLC), 0)
    repeat = cells == lax.broadcasted_iota(jnp.int32, (SUB, SUB * POLC), 1) // POLC
    taper[...] = jnp.dot(
        gain[...],
        jnp.where(repeat, 1.0, 0.0),
        precision=lax.Precision.HIGHEST,
        preferred_element_type=jnp.float32,
    )

    def send(owner, _):
        slots = lax.broadcasted_iota(jnp.int32, (chunk, rows), 0) + owner * chunk
        pick = jnp.where(slots == dest[...], 1.0, 0.0).astype(jnp.bfloat16)
        out[owner] = lax.dot_general(
            feat[...], pick, NT, preferred_element_type=jnp.float32
        ).astype(jnp.bfloat16)
        return 0

    lax.fori_loop(0, owners, send, 0)


def spread(cell, taps):
    rows = lax.broadcasted_iota(jnp.int32, taps.shape, 0) - cell
    parts = []
    for start in range(0, SUB, ROWS):
        delta = rows + start
        weight = jnp.take_along_axis(taps, delta & (ROWS - 1), axis=0)
        parts.append(jnp.where((delta >= 0) & (delta < ROWS), weight, 0.0))
    return jnp.concatenate(parts, axis=0)


def grid_chunk(slot_cap, chunk, channels, lane, feat, table, total, left, right):
    covered = min(BLK_DEV, LANES // slot_cap)
    first = lane % chunk // slot_cap
    columns = channels * POLC
    lanes = lax.broadcasted_iota(jnp.int32, (SUB, LANES), 1)
    block = (lane + lanes) % chunk // slot_cap - first
    samples = feat[:columns, :].astype(jnp.float32)
    codes = feat[columns:, :].astype(jnp.float32).astype(jnp.int32)
    lookup = table[...]
    part = jnp.zeros((covered * SUB, SUB * POLC), jnp.float32)
    for h in range(channels):
        sample = samples[h * POLC : (h + 1) * POLC, :]
        cell_u = codes[h : h + 1, :]
        cell_v = codes[channels + h : channels + h + 1, :]
        row_u = codes[2 * channels + h : 2 * channels + h + 1, :]
        row_v = codes[3 * channels + h : 3 * channels + h + 1, :]
        taps_u = jnp.take_along_axis(lookup, jnp.broadcast_to(row_u, (8, LANES)), axis=1)
        taps_v = jnp.take_along_axis(lookup, jnp.broadcast_to(row_v, (8, LANES)), axis=1)
        weight_u = spread(cell_u, taps_u)
        weight_v = spread(cell_v, taps_v)
        here = pl.ds(h * LANES, LANES)
        weighted = weight_u[:, None, :] * sample[None, :, :]
        right[:, here] = weighted.reshape(SUB * POLC, LANES).astype(jnp.bfloat16)
        for b in range(covered):
            left[pl.ds(b * SUB, SUB), here] = jnp.where(block == b, weight_v, 0.0).astype(
                jnp.bfloat16
            )
        if (h + 1) % GROUP == 0:
            group = pl.ds((h + 1 - GROUP) * LANES, GROUP * LANES)
            part = part + lax.dot_general(
                left[:, group], right[:, group], NT, preferred_element_type=jnp.float32
            )
    place = pl.ds(pl.multiple_of(first * SUB, SUB), covered * SUB)
    total[place, :] = total[place, :] + part


def grid_kernel(slot_cap, chunk, channels, feat, table, taper, out, total, left, right):
    step = pl.program_id(0)

    @pl.when(step == 0)
    def _():
        total[...] = jnp.zeros_like(total)

    grid_chunk(
        slot_cap, chunk, channels, step * LANES, feat[0], table, total, left, right
    )

    @pl.when(step == pl.num_programs(0) - 1)
    def _():
        for b in range(BLK_DEV):
            out[b] = (total[pl.ds(b * SUB, SUB), :] * taper[...]).astype(jnp.bfloat16)


def move_grid_kernel(
    slot_cap, channels, send, table, taper, out, moved, total, left, right, own_sem, to_sem, at_sem
):
    count, features, chunk = send.shape
    v, t = lax.axis_index("vis"), lax.axis_index("tile")
    barrier = pltpu.get_barrier_semaphore()
    for k in range(1, count):
        pl.semaphore_signal(barrier, inc=1, device_id=((v + k) % count, t), device_id_type=MESH)
    pl.semaphore_wait(barrier, count - 1)

    def copy(k):
        return pltpu.make_async_remote_copy(
            src_ref=send.at[(v + k) % count],
            dst_ref=moved.at[v],
            send_sem=to_sem.at[k],
            recv_sem=at_sem.at[k],
            device_id=((v + k) % count, t),
            device_id_type=MESH,
        )

    own = pltpu.make_async_copy(send.at[v], moved.at[v], own_sem.at[0])
    own.start()
    for k in range(1, count):
        copy(k).start()
    total[...] = jnp.zeros_like(total)
    own.wait()

    def source(k, _):
        @pl.when(k > 0)
        def _():
            copy(k).wait_recv()

        origin = (v + count - k) % count

        def part(piece, _):
            lane = pl.multiple_of(piece * LANES, LANES)
            grid_chunk(
                slot_cap,
                chunk,
                channels,
                lane,
                moved[origin, :, pl.ds(lane, LANES)],
                table,
                total,
                left,
                right,
            )
            return 0

        lax.fori_loop(0, chunk // LANES, part, 0)
        return 0

    lax.fori_loop(0, count, source, 0)
    for b in range(BLK_DEV):
        out[b] = (total[pl.ds(b * SUB, SUB), :] * taper[...]).astype(jnp.bfloat16)
    for k in range(1, count):
        copy(k).wait_send()


def slot_kernel(tiles, anchors, subs, out, meta):
    slots = out.shape[0]
    out[...] = jnp.zeros_like(out)
    lanes = lax.broadcasted_iota(jnp.int32, meta.shape, 1)
    places = jnp.full(meta.shape, -FAR, jnp.int32)
    for b in range(BLK_DEV):
        slot = tiles[b, 0] * SCAP
        for before in range(b):
            slot = slot + jnp.where(tiles[before, 0] == tiles[b, 0], 1, 0)
        out[slot] = subs[b]
        places = jnp.where(lanes == slot, anchors[b, 0], places)
        places = jnp.where(lanes == slots + slot, anchors[b, 1], places)
    meta[...] = places


def gather_kernel(subs, meta, out, meta_out, own_sem, near_send, near_recv, far_send, far_recv):
    count = out.shape[0]
    width = out.shape[1]
    v, t = lax.axis_index("vis"), lax.axis_index("tile")
    half = count // 2
    spot = v // 2 * (1 - v % 2) + (count - 1 - v // 2) * (v % 2)

    def member(position):
        position = (position + 2 * count) % count
        back = position // half
        return (1 - back) * 2 * position + back * (2 * (count - 1 - position) + 1)

    barrier = pltpu.get_barrier_semaphore()
    for side in (1, -1):
        pl.semaphore_signal(
            barrier, inc=1, device_id=(member(spot + side), t), device_id_type=MESH
        )
    for k in range(1, width):
        pl.semaphore_signal(barrier, inc=1, device_id=(v, (t + k) % width), device_id_type=MESH)
    pl.semaphore_wait(barrier, 1 + width)

    def near(k):
        chunk = pl.ds((t + k) % width, 1)
        pairs = ((subs.at[chunk], out.at[v, pl.ds(t, 1)]), (meta, meta_out.at[v, t]))
        return [
            pltpu.make_async_remote_copy(
                src_ref=src,
                dst_ref=dst,
                send_sem=near_send.at[2 * k + i],
                recv_sem=near_recv.at[2 * k + i],
                device_id=(v, (t + k) % width),
                device_id_type=MESH,
            )
            for i, (src, dst) in enumerate(pairs)
        ]

    def own():
        pairs = ((subs.at[pl.ds(t, 1)], out.at[v, pl.ds(t, 1)]), (meta, meta_out.at[v, t]))
        return [
            pltpu.make_async_copy(src, dst, own_sem.at[i]) for i, (src, dst) in enumerate(pairs)
        ]

    def far(k, step):
        side = 1 - 2 * (k % 2)
        origin = member(spot - side * step)
        source = (t + width - k) % width
        refs = (out.at[origin, pl.ds(source, 1)], meta_out.at[origin, source])
        return [
            pltpu.make_async_remote_copy(
                src_ref=ref,
                dst_ref=ref,
                send_sem=far_send.at[(step * width + k) * 2 + i],
                recv_sem=far_recv.at[(step * width + k) * 2 + i],
                device_id=(member(spot + side), t),
                device_id_type=MESH,
            )
            for i, ref in enumerate(refs)
        ]

    for copy in own():
        copy.start()
    for k in range(1, width):
        for copy in near(k):
            copy.start()
    for copy in own():
        copy.wait()
    for k in range(width):
        if k:
            for copy in near(k):
                copy.wait_recv()
        for copy in far(k, 0):
            copy.start()

    def forward(step, _):
        for k in range(width):
            for copy in far(k, step - 1):
                copy.wait_recv()
            for copy in far(k, step):
                copy.start()
        return 0

    lax.fori_loop(1, count - 1, forward, 0)
    for k in range(width):
        for copy in far(k, count - 2):
            copy.wait_recv()
    for k in range(1, width):
        for copy in near(k):
            copy.wait_send()

    def sent(step, _):
        for k in range(width):
            for copy in far(k, step):
                copy.wait_send()
        return 0

    lax.fori_loop(0, count - 1, sent, 0)


def place_kernel(tile_slots, meta, subs, out, canvas):
    v, t = lax.axis_index("vis"), lax.axis_index("tile")
    step = pl.program_id(0)
    slots = subs.shape[1]
    height = out.shape[1]
    width = out.shape[2]
    span = SUB * POLC

    @pl.when(step == 0)
    def _():
        canvas[...] = jnp.zeros_like(canvas)

    def add_one(slot, _):
        source = step * (slots // tile_slots) + slot // tile_slots
        lane = t * tile_slots + slot % tile_slots
        low = meta[source, lane] - v * height + SUB
        column = meta[source, slots + lane] * POLC

        @pl.when((low > 0) & (low < height + SUB))
        def _():
            sub = subs[0, slot].astype(jnp.float32)
            sub = jnp.concatenate([sub, jnp.zeros((SUB, LANES), jnp.float32)], axis=1)
            sub = pltpu.roll(sub, column % LANES, 1)
            sub = jnp.concatenate([sub, jnp.zeros((ROWS, span + LANES), jnp.float32)], axis=0)
            sub = pltpu.roll(sub, low % ROWS, 0)
            top = pl.multiple_of(low // ROWS * ROWS, ROWS)
            base = pl.multiple_of(column // LANES * LANES, LANES)
            tile = slot % tile_slots // SCAP
            here = (tile, pl.ds(top, SUB + ROWS), pl.ds(base, span + LANES))
            canvas[here] = canvas[here] + sub

        return 0

    lax.fori_loop(0, slots, add_one, 0)

    @pl.when(step == pl.num_programs(0) - 1)
    def _():
        out[...] = canvas[:, pl.ds(SUB, height), pl.ds(0, width)]


def on_device(
    vis_data,
    u_cell,
    v_cell,
    u_frac,
    v_frac,
    w_plane,
    block_route,
    kernel_taps,
    taper_gain,
    sub_tile,
    sub_anchor,
):
    vis_count = lax.axis_size("vis")
    tile_width = lax.axis_size("tile")
    gt_dev = GT // tile_width
    rows, columns = vis_data.shape
    channels = u_cell.shape[0]
    slot_cap = max(2, 2 * rows // (BLK_DEV * vis_count))
    chunk = BLK_DEV * slot_cap
    features = columns + 4 * channels
    per_owner = gt_dev * SCAP
    slots = tile_width * per_owner
    height = TS // vis_count
    width = TS * POLC

    send, table, taper = pl.pallas_call(
        functools.partial(dispatch_kernel, slot_cap),
        out_shape=[
            jax.ShapeDtypeStruct((vis_count, features, chunk), jnp.bfloat16),
            jax.ShapeDtypeStruct((ROWS, LANES), jnp.float32),
            jax.ShapeDtypeStruct((SUB, SUB * POLC), jnp.float32),
        ],
        scratch_shapes=[
            pltpu.VMEM((features, rows), jnp.bfloat16),
            pltpu.VMEM((1, rows), jnp.int32),
        ],
        name="dispatch",
    )(
        vis_data,
        u_cell,
        v_cell,
        u_frac,
        v_frac,
        w_plane,
        block_route.reshape(1, rows),
        kernel_taps,
        taper_gain,
    )
    covered = min(BLK_DEV, LANES // slot_cap)
    vmem = pl.BlockSpec(memory_space=pltpu.VMEM)
    work = [
        pltpu.VMEM((BLK_DEV * SUB, SUB * POLC), jnp.float32),
        pltpu.VMEM((covered * SUB, channels * LANES), jnp.bfloat16),
        pltpu.VMEM((SUB * POLC, channels * LANES), jnp.bfloat16),
    ]
    gridded = jax.ShapeDtypeStruct((BLK_DEV, SUB, SUB * POLC), jnp.bfloat16)
    if chunk % LANES == 0:
        subs = pl.pallas_call(
            functools.partial(move_grid_kernel, slot_cap, channels),
            in_specs=[vmem, vmem, vmem],
            out_specs=vmem,
            out_shape=gridded,
            scratch_shapes=[pltpu.VMEM(send.shape, jnp.bfloat16)]
            + work
            + [
                pltpu.SemaphoreType.DMA((1,)),
                pltpu.SemaphoreType.DMA((vis_count,)),
                pltpu.SemaphoreType.DMA((vis_count,)),
            ],
            compiler_params=pltpu.CompilerParams(collective_id=1, has_side_effects=True),
            name="move_grid",
        )(send, table, taper)
    else:
        moved = lax.all_to_all(send, "vis", split_axis=0, concat_axis=0, tiled=True)
        moved = jnp.transpose(moved, (1, 0, 2)).reshape(1, features, vis_count * chunk)
        subs = pl.pallas_call(
            functools.partial(grid_kernel, slot_cap, chunk, channels),
            grid=(moved.shape[2] // LANES,),
            in_specs=[
                pl.BlockSpec((1, features, LANES), lambda s: (0, 0, s)),
                pl.BlockSpec(table.shape, lambda s: (0, 0)),
                pl.BlockSpec(taper.shape, lambda s: (0, 0)),
            ],
            out_specs=pl.BlockSpec(gridded.shape, lambda s: (0, 0, 0)),
            out_shape=gridded,
            scratch_shapes=work,
            name="grid",
        )(moved, table, taper)
    scalars = pl.BlockSpec(memory_space=pltpu.SMEM)
    subs, meta = pl.pallas_call(
        slot_kernel,
        in_specs=[scalars, scalars, vmem],
        out_specs=[vmem, vmem],
        out_shape=[
            jax.ShapeDtypeStruct((slots, SUB, SUB * POLC), jnp.bfloat16),
            jax.ShapeDtypeStruct((1, LANES), jnp.int32),
        ],
        name="slot",
    )(sub_tile, sub_anchor, subs)
    hops = (vis_count - 1) * tile_width * 2
    subs, meta = pl.pallas_call(
        gather_kernel,
        in_specs=[vmem, vmem],
        out_specs=[vmem, vmem],
        out_shape=[
            jax.ShapeDtypeStruct(
                (vis_count, tile_width, per_owner, SUB, SUB * POLC), jnp.bfloat16
            ),
            jax.ShapeDtypeStruct((vis_count, tile_width, 1, LANES), jnp.int32),
        ],
        scratch_shapes=[
            pltpu.SemaphoreType.DMA((2,)),
            pltpu.SemaphoreType.DMA((2 * tile_width,)),
            pltpu.SemaphoreType.DMA((2 * tile_width,)),
            pltpu.SemaphoreType.DMA((hops,)),
            pltpu.SemaphoreType.DMA((hops,)),
        ],
        compiler_params=pltpu.CompilerParams(collective_id=0, has_side_effects=True),
        name="gather",
    )(subs.reshape(tile_width, per_owner, SUB, SUB * POLC), meta)
    subs = subs.reshape(vis_count, slots, SUB, SUB * POLC)
    meta = meta.reshape(vis_count * tile_width, LANES)
    return pl.pallas_call(
        functools.partial(place_kernel, per_owner),
        grid_spec=pltpu.PrefetchScalarGridSpec(
            num_scalar_prefetch=1,
            grid=(vis_count,),
            in_specs=[pl.BlockSpec((1, slots, SUB, SUB * POLC), lambda s, *_: (s, 0, 0, 0))],
            out_specs=pl.BlockSpec((gt_dev, height, width), lambda s, *_: (0, 0, 0)),
            scratch_shapes=[
                pltpu.VMEM((gt_dev, -(-height // ROWS) * ROWS + 2 * SUB + ROWS, width + LANES), jnp.float32),
            ],
        ),
        out_shape=jax.ShapeDtypeStruct((gt_dev, height, width), jnp.float32),
        name="place",
    )(meta, subs)


def solution(mesh):
    placed = (
        P(("vis", "tile"), None),
        P(None, ("vis", "tile")),
        P(None, ("vis", "tile")),
        P(None, ("vis", "tile")),
        P(None, ("vis", "tile")),
        P(None, ("vis", "tile")),
        P(("vis", "tile"), None),
        P(),
        P(),
        P(("vis", "tile"), None),
        P(("vis", "tile"), None),
    )
    return jax.shard_map(
        on_device, mesh=mesh, in_specs=placed, out_specs=P("tile", "vis", None), check_vma=False
    )
```

```python
import functools

import jax
import jax.numpy as jnp
from jax import lax
from jax.experimental import pallas as pl
from jax.experimental.pallas import tpu as pltpu
from jax.sharding import PartitionSpec as P

BLK_DEV = 8
SUB = 32
POLC = 8
TAPS = 7
OS = 16
TS = 256
GT = 8
SCAP = 2
LANES = 128
ROWS = 8
GROUP = 4
FAR = 1 << 20
MESH = pl.DeviceIdType.MESH
NT = (((1,), (1,)), ((), ()))


def dispatch_kernel(
    slot_cap, vis, u_cell, v_cell, u_frac, v_frac, w_plane, route, taps, gain, out, table, taper, feat, dest
):
    rows = vis.shape[0]
    columns = vis.shape[1]
    channels = u_cell.shape[0]
    owners, _, chunk = out.shape
    groups = owners * BLK_DEV
    feat[pl.ds(0, columns), :] = vis[...].astype(jnp.float32).T.astype(jnp.bfloat16)
    plane = w_plane[...] * OS
    codes = (u_cell[...], v_cell[...], plane + u_frac[...], plane + v_frac[...])
    for place, code in enumerate(codes):
        feat[pl.ds(columns + place * channels, channels), :] = code.astype(jnp.float32).astype(
            jnp.bfloat16
        )
    names = route[...]
    mine = lax.broadcasted_iota(jnp.int32, (groups, rows), 0) == names
    onehot = jnp.where(mine, 1.0, 0.0)
    earlier = lax.broadcasted_iota(jnp.int32, (rows, rows), 0) < lax.broadcasted_iota(
        jnp.int32, (rows, rows), 1
    )
    before = jnp.dot(
        onehot.astype(jnp.bfloat16),
        jnp.where(earlier, 1.0, 0.0).astype(jnp.bfloat16),
        preferred_element_type=jnp.float32,
    )
    rank = jnp.sum(onehot * before, axis=0, keepdims=True).astype(jnp.int32)
    dest[...] = names * slot_cap + rank

    turn = lax.broadcasted_iota(jnp.int32, (ROWS, TAPS), 0) == lax.broadcasted_iota(
        jnp.int32, (ROWS, TAPS), 1
    )
    table[...] = lax.dot_general(
        jnp.where(turn, 1.0, 0.0).astype(jnp.bfloat16),
        taps[...].astype(jnp.bfloat16),
        NT,
        preferred_element_type=jnp.float32,
    )
    cells = lax.broadcasted_iota(jnp.int32, (SUB, SUB * POLC), 0)
    repeat = cells == lax.broadcasted_iota(jnp.int32, (SUB, SUB * POLC), 1) // POLC
    taper[...] = jnp.dot(
        gain[...],
        jnp.where(repeat, 1.0, 0.0),
        precision=lax.Precision.HIGHEST,
        preferred_element_type=jnp.float32,
    )

    def send(owner, _):
        slots = lax.broadcasted_iota(jnp.int32, (chunk, rows), 0) + owner * chunk
        pick = jnp.where(slots == dest[...], 1.0, 0.0).astype(jnp.bfloat16)
        out[owner] = lax.dot_general(
            feat[...], pick, NT, preferred_element_type=jnp.float32
        ).astype(jnp.bfloat16)
        return 0

    lax.fori_loop(0, owners, send, 0)


def spread(cell, taps):
    rows = lax.broadcasted_iota(jnp.int32, taps.shape, 0) - cell
    parts = []
    for start in range(0, SUB, ROWS):
        delta = rows + start
        weight = jnp.take_along_axis(taps, delta & (ROWS - 1), axis=0)
        parts.append(jnp.where((delta >= 0) & (delta < ROWS), weight, 0.0))
    return jnp.concatenate(parts, axis=0)


def grid_chunk(slot_cap, chunk, channels, lane, feat, table, total, left, right):
    covered = min(BLK_DEV, LANES // slot_cap)
    first = lane % chunk // slot_cap
    columns = channels * POLC
    lanes = lax.broadcasted_iota(jnp.int32, (SUB, LANES), 1)
    block = (lane + lanes) % chunk // slot_cap - first
    samples = feat[:columns, :].astype(jnp.float32)
    codes = feat[columns:, :].astype(jnp.float32).astype(jnp.int32)
    lookup = table[...]
    part = jnp.zeros((covered * SUB, SUB * POLC), jnp.float32)
    for h in range(channels):
        sample = samples[h * POLC : (h + 1) * POLC, :]
        cell_u = codes[h : h + 1, :]
        cell_v = codes[channels + h : channels + h + 1, :]
        row_u = codes[2 * channels + h : 2 * channels + h + 1, :]
        row_v = codes[3 * channels + h : 3 * channels + h + 1, :]
        taps_u = jnp.take_along_axis(lookup, jnp.broadcast_to(row_u, (8, LANES)), axis=1)
        taps_v = jnp.take_along_axis(lookup, jnp.broadcast_to(row_v, (8, LANES)), axis=1)
        weight_u = spread(cell_u, taps_u)
        weight_v = spread(cell_v, taps_v)
        here = pl.ds(h * LANES, LANES)
        weighted = weight_u[:, None, :] * sample[None, :, :]
        right[:, here] = weighted.reshape(SUB * POLC, LANES).astype(jnp.bfloat16)
        for b in range(covered):
            left[pl.ds(b * SUB, SUB), here] = jnp.where(block == b, weight_v, 0.0).astype(
                jnp.bfloat16
            )
        if (h + 1) % GROUP == 0:
            group = pl.ds((h + 1 - GROUP) * LANES, GROUP * LANES)
            part = part + lax.dot_general(
                left[:, group], right[:, group], NT, preferred_element_type=jnp.float32
            )
    place = pl.ds(pl.multiple_of(first * SUB, SUB), covered * SUB)
    total[place, :] = total[place, :] + part


def grid_kernel(slot_cap, chunk, channels, feat, table, taper, out, total, left, right):
    step = pl.program_id(0)

    @pl.when(step == 0)
    def _():
        total[...] = jnp.zeros_like(total)

    grid_chunk(
        slot_cap, chunk, channels, step * LANES, feat[0], table, total, left, right
    )

    @pl.when(step == pl.num_programs(0) - 1)
    def _():
        for b in range(BLK_DEV):
            out[b] = (total[pl.ds(b * SUB, SUB), :] * taper[...]).astype(jnp.bfloat16)


def move_grid_kernel(
    slot_cap, channels, send, table, taper, out, moved, total, left, right, own_sem, to_sem, at_sem
):
    count, features, chunk = send.shape
    v, t = lax.axis_index("vis"), lax.axis_index("tile")
    barrier = pltpu.get_barrier_semaphore()
    for k in range(1, count):
        pl.semaphore_signal(barrier, inc=1, device_id=((v + k) % count, t), device_id_type=MESH)
    pl.semaphore_wait(barrier, count - 1)

    def copy(k):
        return pltpu.make_async_remote_copy(
            src_ref=send.at[(v + k) % count],
            dst_ref=moved.at[v],
            send_sem=to_sem.at[k],
            recv_sem=at_sem.at[k],
            device_id=((v + k) % count, t),
            device_id_type=MESH,
        )

    own = pltpu.make_async_copy(send.at[v], moved.at[v], own_sem.at[0])
    own.start()
    for k in range(1, count):
        copy(k).start()
    total[...] = jnp.zeros_like(total)
    own.wait()

    def source(k, _):
        @pl.when(k > 0)
        def _():
            copy(k).wait_recv()

        origin = (v + count - k) % count

        def part(piece, _):
            lane = pl.multiple_of(piece * LANES, LANES)
            grid_chunk(
                slot_cap,
                chunk,
                channels,
                lane,
                moved[origin, :, pl.ds(lane, LANES)],
                table,
                total,
                left,
                right,
            )
            return 0

        lax.fori_loop(0, chunk // LANES, part, 0)
        return 0

    lax.fori_loop(0, count, source, 0)
    for b in range(BLK_DEV):
        out[b] = (total[pl.ds(b * SUB, SUB), :] * taper[...]).astype(jnp.bfloat16)
    for k in range(1, count):
        copy(k).wait_send()


def slot_kernel(tiles, anchors, subs, out, meta):
    slots = out.shape[0]
    out[...] = jnp.zeros_like(out)
    lanes = lax.broadcasted_iota(jnp.int32, meta.shape, 1)
    places = jnp.full(meta.shape, -FAR, jnp.int32)
    for b in range(BLK_DEV):
        slot = tiles[b, 0] * SCAP
        for before in range(b):
            slot = slot + jnp.where(tiles[before, 0] == tiles[b, 0], 1, 0)
        out[slot] = subs[b]
        places = jnp.where(lanes == slot, anchors[b, 0], places)
        places = jnp.where(lanes == slots + slot, anchors[b, 1], places)
    meta[...] = places


def gather_kernel(subs, meta, out, meta_out, own_sem, near_send, near_recv, far_send, far_recv):
    count = out.shape[0]
    width = out.shape[1]
    v, t = lax.axis_index("vis"), lax.axis_index("tile")
    half = count // 2
    spot = v // 2 * (1 - v % 2) + (count - 1 - v // 2) * (v % 2)

    def member(position):
        position = (position + 2 * count) % count
        back = position // half
        return (1 - back) * 2 * position + back * (2 * (count - 1 - position) + 1)

    barrier = pltpu.get_barrier_semaphore()
    for side in (1, -1):
        pl.semaphore_signal(
            barrier, inc=1, device_id=(member(spot + side), t), device_id_type=MESH
        )
    for k in range(1, width):
        pl.semaphore_signal(barrier, inc=1, device_id=(v, (t + k) % width), device_id_type=MESH)
    pl.semaphore_wait(barrier, 1 + width)

    def near(k):
        chunk = pl.ds((t + k) % width, 1)
        pairs = ((subs.at[chunk], out.at[v, pl.ds(t, 1)]), (meta, meta_out.at[v, t]))
        return [
            pltpu.make_async_remote_copy(
                src_ref=src,
                dst_ref=dst,
                send_sem=near_send.at[2 * k + i],
                recv_sem=near_recv.at[2 * k + i],
                device_id=(v, (t + k) % width),
                device_id_type=MESH,
            )
            for i, (src, dst) in enumerate(pairs)
        ]

    def own():
        pairs = ((subs.at[pl.ds(t, 1)], out.at[v, pl.ds(t, 1)]), (meta, meta_out.at[v, t]))
        return [
            pltpu.make_async_copy(src, dst, own_sem.at[i]) for i, (src, dst) in enumerate(pairs)
        ]

    def far(k, step):
        source = (t + width - k) % width
        cut = out.shape[2] // 2
        copies = []
        for i in range(3):
            side = 1 - 2 * (i % 2)
            origin = member(spot - side * step)
            if i < 2:
                ref = out.at[origin, source, pl.ds(i * cut, cut)]
            else:
                ref = meta_out.at[origin, source]
            copies.append(
                pltpu.make_async_remote_copy(
                    src_ref=ref,
                    dst_ref=ref,
                    send_sem=far_send.at[(step * width + k) * 3 + i],
                    recv_sem=far_recv.at[(step * width + k) * 3 + i],
                    device_id=(member(spot + side), t),
                    device_id_type=MESH,
                )
            )
        return copies

    for copy in own():
        copy.start()
    for k in range(1, width):
        for copy in near(k):
            copy.start()
    for copy in own():
        copy.wait()
    for k in range(width):
        if k:
            for copy in near(k):
                copy.wait_recv()
        for copy in far(k, 0):
            copy.start()

    def forward(step, _):
        for k in range(width):
            for landed, copy in zip(far(k, step - 1), far(k, step)):
                landed.wait_recv()
                copy.start()
        return 0

    lax.fori_loop(1, count - 1, forward, 0)
    for k in range(width):
        for copy in far(k, count - 2):
            copy.wait_recv()
    for k in range(1, width):
        for copy in near(k):
            copy.wait_send()

    def sent(step, _):
        for k in range(width):
            for copy in far(k, step):
                copy.wait_send()
        return 0

    lax.fori_loop(0, count - 1, sent, 0)


def place_kernel(tile_slots, meta, subs, out, canvas):
    v, t = lax.axis_index("vis"), lax.axis_index("tile")
    step = pl.program_id(0)
    slots = subs.shape[1]
    height = out.shape[1]
    width = out.shape[2]
    span = SUB * POLC

    @pl.when(step == 0)
    def _():
        canvas[...] = jnp.zeros_like(canvas)

    def add_source(near, _):
        source = step * (slots // tile_slots) + near
        for slot in range(tile_slots):
            lane = t * tile_slots + slot
            low = meta[source, lane] - v * height + SUB
            column = meta[source, slots + lane] * POLC

            @pl.when((low > 0) & (low < height + SUB))
            def _():
                sub = subs[0, near * tile_slots + slot].astype(jnp.float32)
                sub = jnp.concatenate([sub, jnp.zeros((SUB, LANES), jnp.float32)], axis=1)
                sub = pltpu.roll(sub, column % LANES, 1)
                sub = jnp.concatenate([sub, jnp.zeros((ROWS, span + LANES), jnp.float32)], axis=0)
                sub = pltpu.roll(sub, low % ROWS, 0)
                top = pl.multiple_of(low // ROWS * ROWS, ROWS)
                base = pl.multiple_of(column // LANES * LANES, LANES)
                here = (slot // SCAP, pl.ds(top, SUB + ROWS), pl.ds(base, span + LANES))
                canvas[here] = canvas[here] + sub

        return 0

    lax.fori_loop(0, slots // tile_slots, add_source, 0)

    @pl.when(step == pl.num_programs(0) - 1)
    def _():
        out[...] = canvas[:, pl.ds(SUB, height), pl.ds(0, width)]


def on_device(
    vis_data,
    u_cell,
    v_cell,
    u_frac,
    v_frac,
    w_plane,
    block_route,
    kernel_taps,
    taper_gain,
    sub_tile,
    sub_anchor,
):
    vis_count = lax.axis_size("vis")
    tile_width = lax.axis_size("tile")
    gt_dev = GT // tile_width
    rows, columns = vis_data.shape
    channels = u_cell.shape[0]
    slot_cap = max(2, 2 * rows // (BLK_DEV * vis_count))
    chunk = BLK_DEV * slot_cap
    features = columns + 4 * channels
    per_owner = gt_dev * SCAP
    slots = tile_width * per_owner
    height = TS // vis_count
    width = TS * POLC

    send, table, taper = pl.pallas_call(
        functools.partial(dispatch_kernel, slot_cap),
        out_shape=[
            jax.ShapeDtypeStruct((vis_count, features, chunk), jnp.bfloat16),
            jax.ShapeDtypeStruct((ROWS, LANES), jnp.float32),
            jax.ShapeDtypeStruct((SUB, SUB * POLC), jnp.float32),
        ],
        scratch_shapes=[
            pltpu.VMEM((features, rows), jnp.bfloat16),
            pltpu.VMEM((1, rows), jnp.int32),
        ],
        name="dispatch",
    )(
        vis_data,
        u_cell,
        v_cell,
        u_frac,
        v_frac,
        w_plane,
        block_route.reshape(1, rows),
        kernel_taps,
        taper_gain,
    )
    covered = min(BLK_DEV, LANES // slot_cap)
    vmem = pl.BlockSpec(memory_space=pltpu.VMEM)
    work = [
        pltpu.VMEM((BLK_DEV * SUB, SUB * POLC), jnp.float32),
        pltpu.VMEM((covered * SUB, channels * LANES), jnp.bfloat16),
        pltpu.VMEM((SUB * POLC, channels * LANES), jnp.bfloat16),
    ]
    gridded = jax.ShapeDtypeStruct((BLK_DEV, SUB, SUB * POLC), jnp.bfloat16)
    if chunk % LANES == 0:
        subs = pl.pallas_call(
            functools.partial(move_grid_kernel, slot_cap, channels),
            in_specs=[vmem, vmem, vmem],
            out_specs=vmem,
            out_shape=gridded,
            scratch_shapes=[pltpu.VMEM(send.shape, jnp.bfloat16)]
            + work
            + [
                pltpu.SemaphoreType.DMA((1,)),
                pltpu.SemaphoreType.DMA((vis_count,)),
                pltpu.SemaphoreType.DMA((vis_count,)),
            ],
            compiler_params=pltpu.CompilerParams(collective_id=1, has_side_effects=True),
            name="move_grid",
        )(send, table, taper)
    else:
        moved = lax.all_to_all(send, "vis", split_axis=0, concat_axis=0, tiled=True)
        moved = jnp.transpose(moved, (1, 0, 2)).reshape(1, features, vis_count * chunk)
        subs = pl.pallas_call(
            functools.partial(grid_kernel, slot_cap, chunk, channels),
            grid=(moved.shape[2] // LANES,),
            in_specs=[
                pl.BlockSpec((1, features, LANES), lambda s: (0, 0, s)),
                pl.BlockSpec(table.shape, lambda s: (0, 0)),
                pl.BlockSpec(taper.shape, lambda s: (0, 0)),
            ],
            out_specs=pl.BlockSpec(gridded.shape, lambda s: (0, 0, 0)),
            out_shape=gridded,
            scratch_shapes=work,
            name="grid",
        )(moved, table, taper)
    scalars = pl.BlockSpec(memory_space=pltpu.SMEM)
    subs, meta = pl.pallas_call(
        slot_kernel,
        in_specs=[scalars, scalars, vmem],
        out_specs=[vmem, vmem],
        out_shape=[
            jax.ShapeDtypeStruct((slots, SUB, SUB * POLC), jnp.bfloat16),
            jax.ShapeDtypeStruct((1, LANES), jnp.int32),
        ],
        name="slot",
    )(sub_tile, sub_anchor, subs)
    hops = (vis_count - 1) * tile_width * 3
    subs, meta = pl.pallas_call(
        gather_kernel,
        in_specs=[vmem, vmem],
        out_specs=[vmem, vmem],
        out_shape=[
            jax.ShapeDtypeStruct(
                (vis_count, tile_width, per_owner, SUB, SUB * POLC), jnp.bfloat16
            ),
            jax.ShapeDtypeStruct((vis_count, tile_width, 1, LANES), jnp.int32),
        ],
        scratch_shapes=[
            pltpu.SemaphoreType.DMA((2,)),
            pltpu.SemaphoreType.DMA((2 * tile_width,)),
            pltpu.SemaphoreType.DMA((2 * tile_width,)),
            pltpu.SemaphoreType.DMA((hops,)),
            pltpu.SemaphoreType.DMA((hops,)),
        ],
        compiler_params=pltpu.CompilerParams(collective_id=0, has_side_effects=True),
        name="gather",
    )(subs.reshape(tile_width, per_owner, SUB, SUB * POLC), meta)
    subs = subs.reshape(vis_count, slots, SUB, SUB * POLC)
    meta = meta.reshape(vis_count * tile_width, LANES)
    return pl.pallas_call(
        functools.partial(place_kernel, per_owner),
        grid_spec=pltpu.PrefetchScalarGridSpec(
            num_scalar_prefetch=1,
            grid=(vis_count,),
            in_specs=[pl.BlockSpec((1, slots, SUB, SUB * POLC), lambda s, *_: (s, 0, 0, 0))],
            out_specs=pl.BlockSpec((gt_dev, height, width), lambda s, *_: (0, 0, 0)),
            scratch_shapes=[
                pltpu.VMEM((gt_dev, -(-height // ROWS) * ROWS + 2 * SUB + ROWS, width + LANES), jnp.float32),
            ],
        ),
        out_shape=jax.ShapeDtypeStruct((gt_dev, height, width), jnp.float32),
        name="place",
    )(meta, subs)


def solution(mesh):
    placed = (
        P(("vis", "tile"), None),
        P(None, ("vis", "tile")),
        P(None, ("vis", "tile")),
        P(None, ("vis", "tile")),
        P(None, ("vis", "tile")),
        P(None, ("vis", "tile")),
        P(("vis", "tile"), None),
        P(),
        P(),
        P(("vis", "tile"), None),
        P(("vis", "tile"), None),
    )
    return jax.shard_map(
        on_device, mesh=mesh, in_specs=placed, out_specs=P("tile", "vis", None), check_vma=False
    )
```
